32 devices in a mesh: tm: 16 (over z, y, x), seq: 2 (over core).
Axes of the slice: x: 2, y: 2, z: 4, core: 2. Of those that a mesh axis runs over, the one named last changes fastest.
Arguments:
- gains: float32 [128, 128, 128], P(('seq', 'tm')), parts along dimension 0, may hold values from -1 to 1
- offsets: float32 [128, 128], P(('seq', 'tm')), parts along dimension 0, may hold values from -8 to 8
- cov_terms: float32 [128, 128, 128], P(('seq', 'tm')), parts along dimension 0, as said below
Outputs:
- smoothed_means: float32 [128, 128], P(('seq', 'tm')), parts along dimension 0
- smoothed_covs: float32 [128, 128, 128], P(('seq', 'tm')), parts along dimension 0
- moments: float32 [256, 128], P('seq'), parts along dimension 0
The draws below stay inside these ranges and needn't reach their ends.
There are 2 independent parts, one for each index of `seq`. The reference program is written for one: setup_inputs(seed, part) draws one part's arguments, and reference() takes and returns one part's arrays. A program takes and returns all parts, laid end to end along the dimension named above; each array names one. Nothing has to cross between parts.
Inputs may be any that keep to these rules, and one draw needn't show every extreme that they name: `cov_terms`: each step's covariance term is symmetric positive definite.
All inputs are finite; a program needn't handle non-finite values.
Results may differ from the reference program's by a relative error of at most 0.00014.
Values sent between devices are 32-bit elements; how exact they have to be, the bound alone decides.
A program may use at most 128 MiB of HBM per device.

```python
import jax
import jax.numpy as jnp
from jax import lax

STATE = 128
WINDOW_COUNT = 64


def rate_table(key):
    starting_element = jax.random.fold_in(key, 7)
    order = jax.random.permutation(jax.random.fold_in(starting_element, 1), STATE)
    slow_count = STATE // 2
    ranking = jnp.argsort(order)
    lagging_indicator = ranking < slow_count
    fast_span = jax.random.uniform(jax.random.fold_in(starting_element, 2), (WINDOW_COUNT, STATE), minval=20.0, maxval=50.0)
    brisk_frequency = jnp.exp(-1.0 / fast_span)
    slow_span = jax.random.uniform(jax.random.fold_in(starting_element, 3), (WINDOW_COUNT, STATE), minval=0.5, maxval=1.0)
    lagging_frequency = jnp.exp(jnp.log(0.5) / WINDOW_COUNT * slow_span)
    recorded_moments = jax.random.randint(jax.random.fold_in(starting_element, 4), (4,), 0, WINDOW_COUNT)
    consecutive_run_span = jnp.where(jnp.any(jnp.arange(WINDOW_COUNT)[:, None] == recorded_moments[None, :], axis=1), 0.6, 1.0)
    measurement_frequency = jnp.where(lagging_indicator[None, :], lagging_frequency * consecutive_run_span[:, None], brisk_frequency)
    return measurement_frequency.astype(jnp.float32)


def frame_table(key):
    raw = jax.random.normal(jax.random.fold_in(key, 11), (WINDOW_COUNT + 1, STATE, STATE), dtype=jnp.float32)

    def one_frame(matrix):
        basis, upper = jnp.linalg.qr(matrix)
        signs = jnp.where(jnp.diagonal(upper) >= 0.0, 1.0, -1.0)
        return basis * signs[None, :]
    return lax.map(one_frame, raw)


def draw_gains(key, part):
    measurement_frequency = rate_table(key)
    snapshot_table = frame_table(key)
    scaled = snapshot_table[:WINDOW_COUNT] * measurement_frequency[:, None, :]
    gain = jnp.einsum('tij,tkj->tik', scaled, snapshot_table[1:], precision=lax.Precision.HIGHEST)
    return gain.astype(jnp.float32)


def draw_offsets(key, part):
    measurement_frequency = rate_table(key)
    snapshot_table = frame_table(key)
    noise = jax.random.truncated_normal(jax.random.fold_in(key, 31), -4.0, 4.0, (WINDOW_COUNT, STATE))
    inner = 2.0 * noise * jnp.sqrt(1.0 - measurement_frequency * measurement_frequency)
    outer = jnp.einsum('tij,tj->ti', snapshot_table[:WINDOW_COUNT], inner, precision=lax.Precision.HIGHEST)
    return jnp.clip(outer, -8.0, 8.0).astype(jnp.float32)


def draw_cov_terms(key, part):
    measurement_frequency = rate_table(key)
    snapshot_table = frame_table(key)
    top_level = 4.0
    level = jnp.exp(jax.random.uniform(jax.random.fold_in(key, 41), (STATE,), minval=jnp.log(0.5), maxval=jnp.log(top_level)))
    jitter = jnp.exp(jax.random.uniform(jax.random.fold_in(key, 42), (WINDOW_COUNT, STATE), minval=jnp.log(0.7), maxval=jnp.log(1.4)))
    diag_part = (1.0 - measurement_frequency * measurement_frequency) * level[None, :] * jitter
    location_list = jax.random.uniform(jax.random.fold_in(key, 43), (WINDOW_COUNT, STATE))
    kernel = jnp.exp(-(location_list[:, :, None] - location_list[:, None, :]) ** 2 / 0.02)
    root = jnp.sqrt(diag_part)
    unit = jnp.eye(STATE, dtype=jnp.float32)
    inner = root[:, :, None] * root[:, None, :] * (0.5 * unit[None] + 0.5 * kernel)
    rotated = jnp.einsum('tij,tjk->tik', snapshot_table[:WINDOW_COUNT], inner, precision=lax.Precision.HIGHEST)
    full = jnp.einsum('tik,tlk->til', rotated, snapshot_table[:WINDOW_COUNT], precision=lax.Precision.HIGHEST)
    full = 0.5 * (full + jnp.swapaxes(full, 1, 2))
    return full.astype(jnp.float32)


def setup_inputs(seed: int = 0, part: int = 0) -> dict:
    key_list = jax.random.split(jax.random.key(seed), 4)
    own_keys = jax.random.split(jax.random.fold_in(key_list[3], part), 4)
    gains = draw_gains(jax.random.fold_in(jax.random.fold_in(key_list[3], part), 71), part)
    offsets = draw_offsets(jax.random.fold_in(jax.random.fold_in(key_list[3], part), 71), part)
    cov_terms = draw_cov_terms(jax.random.fold_in(jax.random.fold_in(key_list[3], part), 71), part)
    return dict(gains=gains, offsets=offsets, cov_terms=cov_terms)


def product(left, right):
    return jnp.dot(left.astype(jnp.float32), right.astype(jnp.float32), precision=lax.Precision.HIGHEST, preferred_element_type=jnp.float32)

def reference(gains, offsets, cov_terms):
    gains = gains.at[WINDOW_COUNT - 1].set(jnp.zeros_like(gains[0]))

    def walk(state_pair, element):
        upcoming_average, cov_next = state_pair
        gain, offset, covariance = element
        mean_now = offset + product(gain, upcoming_average)
        cov_now = covariance + product(product(gain, cov_next), gain.T)
        return ((mean_now, cov_now), (mean_now, cov_now))
    start = (jnp.zeros((STATE,), jnp.float32), jnp.zeros((STATE, STATE), jnp.float32))
    final_pair, outputs = lax.scan(walk, start, (gains, offsets, cov_terms), reverse=True)
    means, covs = outputs
    moments = (jnp.sum(covs, axis=0) + product(means.T, means)) / WINDOW_COUNT
    return (means, covs, moments)
```

```python
import functools

import jax
import jax.numpy as jnp
from jax import lax
from jax.experimental import pallas as pl
from jax.experimental.pallas import tpu as pltpu
from jax.sharding import PartitionSpec as P

F32 = jnp.float32
BF16 = jnp.bfloat16
GROUP = 16


def split(x):
    hi = x.astype(BF16)
    return hi, (x - hi.astype(F32)).astype(BF16)


def left(x):
    hi, lo = split(x)
    return hi, jnp.concatenate([hi, lo], axis=1)


def right(w):
    hi, lo = split(w)
    return jnp.concatenate([hi, hi], axis=0), lo


def mul(x, w):
    hi, both = x
    w_hi, w_lo = w
    return jnp.dot(both, w_hi, preferred_element_type=F32) + jnp.dot(
        hi, w_lo, preferred_element_type=F32
    )


def kernel(
    n, gains, offsets, covs, means_out, covs_out, mom_out,
    psi, mp, snd_psi, snd_mp, rcv_psi, rcv_mp, mom, rs_buf, red, bf_snd, bf_rcv, mom_all,
    ps_s, ps_r, mp_s, mp_r, rs_s, rs_r, bf_s, bf_r, ag_s, ag_r, out_s,
):
    steps, width = gains.shape[0], gains.shape[1]
    me = lax.axis_index("tm")
    rounds = n.bit_length() - 3
    quarter = n // 4
    place = lax.rem(me, GROUP)
    base = me - place
    rows = width // GROUP
    wide = n // GROUP

    def flip(step):
        bit = lax.rem(lax.div(me, step), 2)
        return me + step * (1 - 2 * bit), bit

    peers = [base + lax.rem(place + j, GROUP) for j in range(1, GROUP)]
    far = GROUP
    while far < n:
        peers.append(flip(far)[0])
        far *= 2
    q = lax.div(me, quarter)
    if n > GROUP:
        peers.append(lax.rem(me, quarter) + quarter * (3 - q))
    barrier = pltpu.get_barrier_semaphore()
    for peer in peers:
        pl.semaphore_signal(barrier, inc=1, device_id={"tm": peer}, device_id_type=pl.DeviceIdType.MESH)

    def send(src, dst, s, r, to):
        return pltpu.make_async_remote_copy(
            src_ref=src, dst_ref=dst, send_sem=s, recv_sem=r,
            device_id={"tm": to}, device_id_type=pl.DeviceIdType.MESH,
        )

    for t in reversed(range(steps)):
        gain = gains[t]
        if t == steps - 1:
            gain = jnp.where(me == n - 1, jnp.zeros_like(gain), gain)
        gain_t = gain.T
        offset = jnp.broadcast_to(offsets[t : t + 1, :], (8, width))
        if t == steps - 1:
            psi[t] = gain_t
            mp[t, :width] = covs[t]
            mp[t, width:] = offset
        else:
            x = mul(left(jnp.concatenate([psi[t + 1], mp[t + 1]], axis=0)), right(gain_t))
            psi[t] = x[:width]
            mp[t, width:] = x[2 * width :] + offset
            mp[t, :width] = covs[t] + mul(left(gain), right(x[width : 2 * width]))

    def compose(e_psi, e_mp, f_psi, f_mp):
        parts = [f_mp] if f_psi is None else [f_mp, f_psi]
        x = mul(left(jnp.concatenate(parts, axis=0)), right(e_psi))
        p = e_mp[:width] + mul(left(e_psi.T), right(x[:width]))
        m = e_mp[width:] + x[width : width + 8]
        return (None if f_psi is None else x[width + 8 :]), p, m

    def absorb(slot, with_gain):
        f_psi = rcv_psi[slot] if with_gain else None
        for t in range(steps):
            new_psi, p, m = compose(psi[t], mp[t], f_psi, rcv_mp[slot])
            if with_gain:
                psi[t] = new_psi
            mp[t, :width] = p
            mp[t, width:] = m

    pl.semaphore_wait(barrier, len(peers))

    snd_psi[0] = psi[0]
    snd_mp[0] = mp[0]
    waits = []
    for k in range(rounds):
        to, bit = flip(1 << k)
        a = send(snd_psi.at[k], rcv_psi.at[k], ps_s.at[k], ps_r.at[k], to)
        b = send(snd_mp.at[k], rcv_mp.at[k], mp_s.at[k], mp_r.at[k], to)
        a.start()
        b.start()
        waits += [a, b]
        if k:
            @pl.when(lax.rem(lax.div(me, 1 << (k - 1)), 2) == 0)
            def _():
                absorb(k - 1, True)
        a.wait_recv()
        b.wait_recv()
        upper = bit == 1
        own_psi, own_mp, got_psi, got_mp = snd_psi[k], snd_mp[k], rcv_psi[k], rcv_mp[k]
        e_psi = jnp.where(upper, got_psi, own_psi)
        f_psi = jnp.where(upper, own_psi, got_psi)
        e_mp = jnp.where(upper, got_mp, own_mp)
        f_mp = jnp.where(upper, own_mp, got_mp)
        new_psi, p, m = compose(e_psi, e_mp, f_psi, f_mp)
        snd_psi[k + 1] = new_psi
        snd_mp[k + 1, :width] = p
        snd_mp[k + 1, width:] = m

    def settle():
        @pl.when(lax.rem(lax.div(me, 1 << (rounds - 1)), 2) == 0)
        def _():
            absorb(rounds - 1, True)

    one, two = rounds, rounds + 1
    down, down2 = lax.rem(me + n - quarter, n), lax.rem(me + n - 2 * quarter, n)
    near_mp = send(snd_mp.at[one], rcv_mp.at[one], mp_s.at[one], mp_r.at[one], down)
    near_psi = send(snd_psi.at[one], rcv_psi.at[one], ps_s.at[one], ps_r.at[one], down)
    top_far = send(snd_mp.at[two], rcv_mp.at[two], mp_s.at[two], mp_r.at[two], down2)
    top_near = send(snd_mp.at[two], rcv_mp.at[two], mp_s.at[two + 1], mp_r.at[two], down)

    @pl.when(q == 3)
    def _():
        near_mp.start()
        settle()
        near_mp.wait_send()

    @pl.when(q == 2)
    def _():
        near_mp.wait_recv()
        unused, p, m = compose(snd_psi[one], snd_mp[one], None, rcv_mp[one])
        snd_mp[two, :width] = p
        snd_mp[two, width:] = m
        top_far.start()
        top_near.start()
        settle()
        absorb(one, False)
        top_far.wait_send()
        top_near.wait_send()

    @pl.when(q == 1)
    def _():
        near_psi.start()
        near_mp.start()
        settle()
        top_near.wait_recv()
        absorb(two, False)
        near_psi.wait_send()
        near_mp.wait_send()

    @pl.when(q == 0)
    def _():
        settle()
        near_psi.wait_recv()
        near_mp.wait_recv()
        absorb(one, True)
        top_far.wait_recv()
        absorb(two, False)

    out_copies = []
    for t in range(steps):
        c = pltpu.make_async_copy(mp.at[t, pl.ds(0, width)], covs_out.at[t], out_s.at[t])
        c.start()
        out_copies.append(c)

    means = jnp.concatenate([mp[t, width : width + 1] for t in range(steps)], axis=0)
    means_out[...] = means
    total = mp[0, :width]
    for t in range(1, steps):
        total = total + mp[t, :width]
    m_hi, m_lo = split(means)
    outer = lambda u, v: lax.dot_general(u, v, (((0,), (0,)), ((), ())), preferred_element_type=F32)
    total = total + (outer(m_hi, m_hi) + (outer(m_hi, m_lo) + outer(m_lo, m_hi)))
    mom[...] = total * (1.0 / (steps * n))

    mine = pl.ds(pl.multiple_of(place * rows, rows), rows)
    scatter = []
    for j in range(1, GROUP):
        to = lax.rem(place + j, GROUP)
        c = send(
            mom.at[pl.ds(pl.multiple_of(to * rows, rows), rows)], rs_buf.at[j - 1],
            rs_s.at[j - 1], rs_r.at[j - 1], base + to,
        )
        c.start()
        scatter.append(c)
    acc = mom[mine, :]
    for j in range(1, GROUP):
        scatter[j - 1].wait_recv()
        acc = acc + rs_buf[j - 1]
    step, k = GROUP, 0
    while step < n:
        bf_snd[k] = acc
        c = send(bf_snd.at[k], bf_rcv.at[k], bf_s.at[k], bf_r.at[k], flip(step)[0])
        c.start()
        c.wait()
        acc = acc + bf_rcv[k]
        step, k = step * 2, k + 1
    red[...] = acc
    gather = []
    for j in range(1, GROUP):
        to = lax.rem(place + j, GROUP)
        c = send(red, mom_all.at[mine], ag_s.at[j - 1], ag_r.at[j - 1], base + to)
        c.start()
        gather.append(c)
    mom_all[mine, :] = acc
    for c in waits + scatter + gather:
        c.wait_send()
    for c in out_copies:
        c.wait()
    for c in gather:
        c.wait_recv()
    mom_out[...] = mom_all[...]


def local(n, gains, offsets, cov_terms):
    steps, width = gains.shape[0], gains.shape[1]
    slots = n.bit_length() - 1
    far = max(1, (n // GROUP).bit_length() - 1)
    rows = width // GROUP
    dma = pltpu.SemaphoreType.DMA
    vmem = pl.BlockSpec(memory_space=pltpu.VMEM)
    return pl.pallas_call(
        functools.partial(kernel, n),
        out_shape=(
            jax.ShapeDtypeStruct((steps, width), F32),
            jax.ShapeDtypeStruct((steps, width, width), F32),
            jax.ShapeDtypeStruct((width, width), F32),
        ),
        in_specs=[vmem] * 3,
        out_specs=(vmem, pl.BlockSpec(memory_space=pl.ANY), vmem),
        scratch_shapes=[
            pltpu.VMEM((steps, width, width), F32),
            pltpu.VMEM((steps, width + 8, width), F32),
            pltpu.VMEM((slots, width, width), F32),
            pltpu.VMEM((slots, width + 8, width), F32),
            pltpu.VMEM((slots, width, width), F32),
            pltpu.VMEM((slots, width + 8, width), F32),
            pltpu.VMEM((width, width), F32),
            pltpu.VMEM((GROUP - 1, rows, width), F32),
            pltpu.VMEM((rows, width), F32),
            pltpu.VMEM((far, rows, width), F32),
            pltpu.VMEM((far, rows, width), F32),
            pltpu.VMEM((width, width), F32),
            dma((slots,)), dma((slots,)), dma((slots + 1,)), dma((slots,)),
            dma((GROUP - 1,)), dma((GROUP - 1,)),
            dma((far,)), dma((far,)),
            dma((GROUP - 1,)), dma((GROUP - 1,)),
            dma((steps,)),
        ],
        compiler_params=pltpu.CompilerParams(collective_id=0, has_side_effects=True),
    )(gains, offsets, cov_terms)


def solution(mesh):
    n = mesh.shape["tm"]
    in_specs = (P(("seq", "tm"), None, None), P(("seq", "tm"), None), P(("seq", "tm"), None, None))
    out_specs = (P(("seq", "tm"), None), P(("seq", "tm"), None, None), P("seq", None))
    return jax.shard_map(
        functools.partial(local, n), mesh=mesh, in_specs=in_specs, out_specs=out_specs, check_vma=False
    )
```

```python
import functools

import jax
import jax.numpy as jnp
from jax import lax
from jax.experimental import pallas as pl
from jax.experimental.pallas import tpu as pltpu
from jax.sharding import PartitionSpec as P

F32 = jnp.float32
BF16 = jnp.bfloat16
PAD = 8
GROUP = 16


def split(x):
    hi = x.astype(BF16)
    return hi, (x - hi.astype(F32)).astype(BF16)


def left(x):
    hi, lo = split(x)
    return hi, jnp.concatenate([hi, lo], axis=1)


def right(w):
    hi, lo = split(w)
    return jnp.concatenate([hi, hi], axis=0), lo


def mul(x, w):
    hi, both = x
    w_hi, w_lo = w
    return jnp.dot(both, w_hi, preferred_element_type=F32) + jnp.dot(
        hi, w_lo, preferred_element_type=F32
    )


def kernel(
    n, gains, offsets, covs, means_out, covs_out, mom_out,
    own, ring, suf, z_snd, z_near, top_snd, top_rcv,
    mom, rs_buf, bf_snd, bf_rcv, red, mom_all, mean_rows,
    ring_s, ring_r, z_s, z_r, rs_s, rs_r, bf_s, bf_r, ag_s, ag_r, out_s,
):
    steps, width = gains.shape[0], gains.shape[1]
    lean = width + PAD
    me = lax.axis_index("tm")
    levels = (n.bit_length() - 1) // 2
    quarter = n // 4
    rows = width // GROUP
    place = lax.rem(me, GROUP)
    base = me - place

    def flip(step):
        return me + step * (1 - 2 * lax.rem(lax.div(me, step), 2))

    def digit_of(stride):
        return lax.rem(lax.div(me, stride), 4)

    def peer(stride, j):
        digit = digit_of(stride)
        return me + stride * (lax.rem(digit + j, 4) - digit)

    peers = [base + lax.rem(place + j, GROUP) for j in range(1, GROUP)]
    peers += [peer(4**l, j) for l in range(2, levels) for j in (1, 2, 3)]
    barrier = pltpu.get_barrier_semaphore()
    for to in peers:
        pl.semaphore_signal(barrier, inc=1, device_id={"tm": to}, device_id_type=pl.DeviceIdType.MESH)

    def send(src, dst, s, r, to):
        return pltpu.make_async_remote_copy(
            src_ref=src, dst_ref=dst, send_sem=s, recv_sem=r,
            device_id={"tm": to}, device_id_type=pl.DeviceIdType.MESH,
        )

    def compose(e, f):
        e_psi = e[lean:]
        x = mul(left(f), right(e_psi))
        p = e[:width] + mul(left(e_psi.T), right(x[:width]))
        out = [p, e[width:lean] + x[width:lean]]
        if f.shape[0] > lean:
            out.append(x[lean:])
        return jnp.concatenate(out, axis=0)

    for t in reversed(range(steps)):
        gain = gains[t]
        if t == steps - 1:
            gain = jnp.where(me == n - 1, jnp.zeros_like(gain), gain)
        offset = jnp.broadcast_to(offsets[t : t + 1, :], (PAD, width))
        element = jnp.concatenate([covs[t], offset, gain.T], axis=0)
        own[t] = element if t == steps - 1 else compose(element, own[t + 1])

    def absorb(f):
        for t in range(steps):
            own[t, : f.shape[0]] = compose(own[t], f)

    pl.semaphore_wait(barrier, len(peers))

    def deferred(l):
        digit = digit_of(4**l)

        @pl.when(digit == 0)
        def _():
            suf[...] = compose(ring[l, 1], suf[...])

        @pl.when(digit == 2)
        def _():
            suf[...] = ring[l, 3]

        @pl.when(digit < 3)
        def _():
            absorb(suf[...])

    sends = []
    total = own[0]
    for l in range(levels - 1):
        digit = digit_of(4**l)
        ring[l, digit] = total
        started = []
        for j in (2, 1, 3):
            c = send(
                ring.at[l, digit], ring.at[l, digit], ring_s.at[l, j - 1], ring_r.at[l, j - 1], peer(4**l, j)
            )
            c.start()
            started.append(c)
        if l:
            deferred(l - 1)
        for j in (1, 2, 3):
            came = lax.rem(digit + 4 - j, 4)
            send(
                ring.at[l, came], ring.at[l, came], ring_s.at[l, j - 1], ring_r.at[l, j - 1], peer(4**l, j)
            ).wait_recv()
        sends += started
        high = compose(ring[l, 2], ring[l, 3])
        total = compose(compose(ring[l, 0], ring[l, 1]), high)
        suf[...] = high
    z_snd[...] = total

    q = lax.div(me, quarter)
    down, down2 = lax.rem(me + n - quarter, n), lax.rem(me + n - 2 * quarter, n)
    part = pl.ds(0, lean)
    near_full = send(z_snd, z_near, z_s.at[0], z_r.at[0], down)
    near_lean = send(z_snd.at[part], z_near.at[part], z_s.at[0], z_r.at[0], down)
    top_far = send(top_snd, top_rcv, z_s.at[1], z_r.at[1], down2)
    top_near = send(top_snd, top_rcv, z_s.at[2], z_r.at[1], down)

    @pl.when(q == 3)
    def _():
        near_lean.start()

    @pl.when(q == 1)
    def _():
        near_full.start()

    deferred(levels - 2)

    @pl.when(q == 3)
    def _():
        near_lean.wait_send()

    @pl.when(q == 2)
    def _():
        near_lean.wait_recv()
        top_snd[...] = compose(z_snd[...], z_near[part, :])
        top_far.start()
        top_near.start()
        absorb(z_near[part, :])
        top_far.wait_send()
        top_near.wait_send()

    @pl.when(q == 0)
    def _():
        near_full.wait_recv()
        absorb(z_near[...])

    @pl.when(q < 2)
    def _():
        top_near.wait_recv()
        absorb(top_rcv[...])

    @pl.when(q == 1)
    def _():
        near_full.wait_send()

    out_copies = []
    for t in range(steps):
        out_copies.append(pltpu.make_async_copy(own.at[t, pl.ds(0, width)], covs_out.at[t], out_s.at[t]))
    means = jnp.concatenate([own[t, width : width + 1] for t in range(steps)], axis=0)
    mean_rows[...] = means
    out_copies.append(pltpu.make_async_copy(mean_rows, means_out, out_s.at[steps]))
    sums = own[0, :width]
    for t in range(1, steps):
        sums = sums + own[t, :width]
    m_hi, m_lo = split(means)
    outer = lambda u, v: lax.dot_general(u, v, (((0,), (0,)), ((), ())), preferred_element_type=F32)
    sums = sums + (outer(m_hi, m_hi) + (outer(m_hi, m_lo) + outer(m_lo, m_hi)))
    mom[...] = sums * (1.0 / (steps * n))

    def group_rows(k):
        return pl.ds(pl.multiple_of(k * rows, rows), rows)

    for j in range(1, GROUP):
        to = lax.rem(place + j, GROUP)
        c = send(mom.at[group_rows(to)], rs_buf.at[j - 1], rs_s.at[j - 1], rs_r.at[j - 1], base + to)
        c.start()
        sends.append(c)
    for c in out_copies:
        c.start()
    acc = mom[group_rows(place), :]
    for c, j in zip(sends[1 - GROUP :], range(1, GROUP)):
        c.wait_recv()
        acc = acc + rs_buf[j - 1]
    k = 0
    while GROUP << k < n:
        bf_snd[k] = acc
        c = send(bf_snd.at[k], bf_rcv.at[k], bf_s.at[k], bf_r.at[k], flip(GROUP << k))
        c.start()
        c.wait()
        acc = acc + bf_rcv[k]
        k += 1
    red[...] = acc
    gather = []
    for j in range(1, GROUP):
        to = lax.rem(place + j, GROUP)
        c = send(red, mom_all.at[group_rows(place)], ag_s.at[j - 1], ag_r.at[j - 1], base + to)
        c.start()
        gather.append(c)
    mom_all[group_rows(place), :] = acc
    for c in sends + gather:
        c.wait_send()
    for c in out_copies:
        c.wait()
    for c in gather:
        c.wait_recv()
    last = pltpu.make_async_copy(mom_all, mom_out, out_s.at[steps + 1])
    last.start()
    last.wait()


def hand_over(a, b, c, a_out, b_out, c_out, sems):
    copies = [
        pltpu.make_async_copy(x, y, sems.at[i])
        for i, (x, y) in enumerate(((b, b_out), (c, c_out), (a, a_out)))
    ]
    for copy in copies:
        copy.start()
    for copy in copies:
        copy.wait()


def local(n, gains, offsets, cov_terms):
    steps, width = gains.shape[0], gains.shape[1]
    levels = (n.bit_length() - 1) // 2
    assert n == 4**levels and levels > 1
    slab, lean, rows = 2 * width + PAD, width + PAD, width // GROUP
    far = max(1, (n // GROUP).bit_length() - 1)
    dma = pltpu.SemaphoreType.DMA
    vmem = pl.BlockSpec(memory_space=pltpu.VMEM)
    any_space = pl.BlockSpec(memory_space=pl.ANY)
    shapes = (
        jax.ShapeDtypeStruct((steps, width), F32),
        jax.ShapeDtypeStruct((steps, width, width), F32),
        jax.ShapeDtypeStruct((width, width), F32),
    )
    results = pl.pallas_call(
        functools.partial(kernel, n),
        out_shape=shapes,
        in_specs=[vmem] * 3,
        out_specs=(any_space,) * 3,
        scratch_shapes=[
            pltpu.VMEM((steps, slab, width), F32),
            pltpu.VMEM((levels - 1, 4, slab, width), F32),
            pltpu.VMEM((slab, width), F32),
            pltpu.VMEM((slab, width), F32),
            pltpu.VMEM((slab, width), F32),
            pltpu.VMEM((lean, width), F32),
            pltpu.VMEM((lean, width), F32),
            pltpu.VMEM((width, width), F32),
            pltpu.VMEM((GROUP - 1, rows, width), F32),
            pltpu.VMEM((far, rows, width), F32),
            pltpu.VMEM((far, rows, width), F32),
            pltpu.VMEM((rows, width), F32),
            pltpu.VMEM((width, width), F32),
            pltpu.VMEM((steps, width), F32),
            dma((levels - 1, 3)), dma((levels - 1, 3)),
            dma((3,)), dma((2,)),
            dma((GROUP - 1,)), dma((GROUP - 1,)),
            dma((far,)), dma((far,)),
            dma((GROUP - 1,)), dma((GROUP - 1,)),
            dma((steps + 2,)),
        ],
        compiler_params=pltpu.CompilerParams(collective_id=0, has_side_effects=True),
    )(gains, offsets, cov_terms)
    return pl.pallas_call(
        hand_over,
        out_shape=shapes,
        in_specs=[vmem] * 3,
        out_specs=(any_space,) * 3,
        scratch_shapes=[dma((3,))],
    )(*results)


def solution(mesh):
    n = mesh.shape["tm"]
    in_specs = (P(("seq", "tm"), None, None), P(("seq", "tm"), None), P(("seq", "tm"), None, None))
    out_specs = (P(("seq", "tm"), None), P(("seq", "tm"), None, None), P("seq", None))
    return jax.shard_map(
        functools.partial(local, n), mesh=mesh, in_specs=in_specs, out_specs=out_specs, check_vma=False
    )
```
